32 devices in a mesh: dp: 16 (over z, y, x), tensor: 2 (over core).
Axes of the slice: x: 2, y: 2, z: 4, core: 2. Of those that a mesh axis runs over, the one named last changes fastest.
Arguments:
- residual_in: float32 [4096, 768], P(('dp', 'tensor')), may hold values from -6 to 6
- out_cotangent: float32 [4096, 768], P(('dp', 'tensor')), may hold values from -6 to 6
- segments: int32 [4096], P('dp'), may hold values from 0 to 4095, as said below
- first_gain: float32 [768], replicated, may hold values from 0.5 to 1.5
- first_bias: float32 [768], replicated, may hold values from -1.25 to 1.25
- second_gain: float32 [768], replicated, may hold values from 0.5 to 1.5
- second_bias: float32 [768], replicated, may hold values from -1.25 to 1.25
- attention_weight: float32 [768, 2304], P('dp', 'tensor'), may hold values from -0.21875 to 0.21875
- attention_bias: float32 [2304], P('tensor'), may hold values from -1.75 to 1.75
- output_weight: float32 [768, 768], P('tensor', 'dp'), may hold values from -1.25 to 1.25
- output_bias: float32 [768], replicated, may hold values from -1.75 to 1.75
- expand_weight: float32 [768, 3072], P('dp', 'tensor'), may hold values from -0.21875 to 0.21875
- expand_bias: float32 [3072], P('tensor'), may hold values from -1.75 to 1.75
- shrink_weight: float32 [3072, 768], P('tensor', 'dp'), may hold values from -0.15625 to 0.15625
- shrink_bias: float32 [768], replicated, may hold values from -1.75 to 1.75
- attention_moment: float32 [768, 2304], P('dp', 'tensor'), may hold values from -192 to 192
- output_moment: float32 [768, 768], P('tensor', 'dp'), may hold values from -192 to 192
- expand_moment: float32 [768, 3072], P('dp', 'tensor'), may hold values from -192 to 192
- shrink_moment: float32 [3072, 768], P('tensor', 'dp'), may hold values from -192 to 192
Outputs:
- block_out: float32 [4096, 768], P(('dp', 'tensor'))
- residual_grad: float32 [4096, 768], P(('dp', 'tensor'))
- first_gain_grad: float32 [768], replicated
- first_bias_grad: float32 [768], replicated
- second_gain_grad: float32 [768], replicated
- second_bias_grad: float32 [768], replicated
- attention_weight_grad: float32 [768, 2304], P('dp', 'tensor')
- attention_bias_grad: float32 [2304], P('tensor')
- output_weight_grad: float32 [768, 768], P('tensor', 'dp')
- output_bias_grad: float32 [768], replicated
- expand_weight_grad: float32 [768, 3072], P('dp', 'tensor')
- expand_bias_grad: float32 [3072], P('tensor')
- shrink_weight_grad: float32 [3072, 768], P('tensor', 'dp')
- shrink_bias_grad: float32 [768], replicated
- first_gain_new: float32 [768], replicated
- first_bias_new: float32 [768], replicated
- second_gain_new: float32 [768], replicated
- second_bias_new: float32 [768], replicated
- attention_weight_new: float32 [768, 2304], P('dp', 'tensor')
- attention_bias_new: float32 [2304], P('tensor')
- output_weight_new: float32 [768, 768], P('tensor', 'dp')
- output_bias_new: float32 [768], replicated
- expand_weight_new: float32 [768, 3072], P('dp', 'tensor')
- expand_bias_new: float32 [3072], P('tensor')
- shrink_weight_new: float32 [3072, 768], P('tensor', 'dp')
- shrink_bias_new: float32 [768], replicated
- attention_moment_new: float32 [768, 2304], P('dp', 'tensor')
- output_moment_new: float32 [768, 768], P('tensor', 'dp')
- expand_moment_new: float32 [768, 3072], P('dp', 'tensor')
- shrink_moment_new: float32 [3072, 768], P('tensor', 'dp')
The draws below stay inside these ranges and needn't reach their ends.
Inputs may be any that keep to these rules, and one draw needn't show every extreme that they name: `segments`: segment numbers never fall along the tokens; each equals the index of its segment's first token, a segment never spans two aligned blocks of 256 tokens, and the last token starts a segment of its own.
All inputs are finite; a program needn't handle non-finite values.
Results may differ from the reference program's by a relative error of at most 0.011.
Values may be sent and summed in bfloat16 or wider, within the bound.
A program may use at most 128 MiB of HBM per device.

```python
import math
import jax
import jax.numpy as jnp
from jax import lax

D = 768
HEADS = 12
HEAD = 64
ROT = 16
FF = 3072
TOK_DEV = 256
NS_ITERS = 4
TOKENS = 4096
N_DP = 16
N_TENSOR = 2


def draw_segments(key, part):
    token_index = jnp.arange(TOKENS, dtype=jnp.int32)
    breaks = jax.random.randint(key, (TOKENS,), 0, max(TOK_DEV // 8, 2)) == 0
    starts = breaks | (token_index % TOK_DEV == 0) | (token_index == TOKENS - 1)
    return lax.cummax(jnp.where(starts, token_index, 0), axis=0).astype(jnp.int32)


def raised(array, own_key, source, target, blocks, factor):
    def block_of(dim):
        return (jnp.arange(array.shape[dim]) // (array.shape[dim] // blocks)).reshape((-1,) + (1,) * (array.ndim - 1 - dim))

    one_side = jax.random.permutation(own_key, blocks)[block_of(target)]
    second = (block_of(target) + blocks // 2) % blocks
    return jnp.where((block_of(source) == one_side) | (block_of(source) == second), factor * array, array)


def block_levels(own_key, dims, shards, low, high):
    def one(axis_at, parts):
        steps = jax.random.uniform(jax.random.fold_in(jax.random.fold_in(own_key, 6), axis_at), (parts,), jnp.float32, low / len(shards), high / len(shards))
        return jnp.repeat(jnp.exp(steps), dims[axis_at] // parts).reshape((-1,) + (1,) * (len(dims) - axis_at - 1))

    level = one(*shards[0])
    for cut in shards[1:]:
        level = level * one(*cut)
    return level


def gaussian(stream_key, shape, scale, reach, cuts=(), kind=jnp.bfloat16):
    level = block_levels(stream_key, shape, cuts, -0.22, 0.18) if cuts else 1.0
    result = jax.random.normal(stream_key, shape, jnp.float32) * scale * level
    return jnp.minimum(jnp.maximum(result, -reach), reach).astype(kind)


def gaussian_with(rng, dims, spread, bound, pieces, heavy, kind=jnp.bfloat16):
    drawn = spread * jax.random.normal(rng, dims, jnp.float32)
    if pieces:
        drawn = drawn * block_levels(rng, dims, pieces, -0.22, 0.18)
    return jnp.clip(raised(drawn, jax.random.fold_in(rng, 3), *heavy), -bound, bound).astype(kind)


def setup_inputs(seed: int = 0) -> dict:
    splits = jax.random.split(jax.random.key(seed), 20)
    residual_in = gaussian_with(splits[0], (TOKENS, D), 1.0, 6.0, ((0, 32),), (0, 1, 32, 2.75), jnp.float32)
    out_cotangent = gaussian_with(splits[1], (TOKENS, D), 1.0, 6.0, ((0, 32),), (0, 1, 32, 2.75), jnp.float32)
    segments = draw_segments(jax.random.fold_in(splits[19], 71), 0)
    first_gain = jnp.clip(1.0 + 0.1 * jax.random.normal(splits[3], (D,), jnp.float32), 0.5, 1.5)
    first_bias = gaussian(splits[4], (D,), 0.2, 1.25, (), jnp.float32)
    second_gain = jnp.clip(1.0 + 0.1 * jax.random.normal(splits[5], (D,), jnp.float32), 0.5, 1.5)
    second_bias = gaussian(splits[6], (D,), 0.2, 1.25, (), jnp.float32)
    attention_weight = gaussian(splits[7], (D, 3 * D), D ** -0.5, 0.21875, ((0, 16), (1, 2)), jnp.float32)
    attention_bias = gaussian(splits[8], (3 * D,), 0.3, 1.75, ((0, 2),), jnp.float32)
    output_weight = gaussian(splits[9], (D, D), (D // 32) ** -0.5, 1.25, ((0, 2), (1, 16)), jnp.float32)
    output_bias = gaussian(splits[10], (D,), 0.3, 1.75, (), jnp.float32)
    expand_weight = gaussian(splits[11], (D, FF), D ** -0.5, 0.21875, ((0, 16), (1, 2)), jnp.float32)
    expand_bias = gaussian(splits[12], (FF,), 0.3, 1.75, ((0, 2),), jnp.float32)
    shrink_weight = gaussian(splits[13], (FF, D), (FF // 2) ** -0.5, 0.15625, ((0, 2), (1, 16)), jnp.float32)
    shrink_bias = gaussian(splits[14], (D,), 0.3, 1.75, (), jnp.float32)
    attention_moment = gaussian(splits[15], (D, 3 * D), 32.0, 192.0, ((0, 16), (1, 2)), jnp.float32)
    output_moment = gaussian(splits[16], (D, D), 32.0, 192.0, ((0, 2), (1, 16)), jnp.float32)
    expand_moment = gaussian(splits[17], (D, FF), 32.0, 192.0, ((0, 16), (1, 2)), jnp.float32)
    shrink_moment = gaussian(splits[18], (FF, D), 32.0, 192.0, ((0, 2), (1, 16)), jnp.float32)
    return dict(residual_in=residual_in, out_cotangent=out_cotangent, segments=segments, first_gain=first_gain, first_bias=first_bias, second_gain=second_gain, second_bias=second_bias, attention_weight=attention_weight, attention_bias=attention_bias, output_weight=output_weight, output_bias=output_bias, expand_weight=expand_weight, expand_bias=expand_bias, shrink_weight=shrink_weight, shrink_bias=shrink_bias, attention_moment=attention_moment, output_moment=output_moment, expand_moment=expand_moment, shrink_moment=shrink_moment)


norm_eps = 1e-05
momentum_rate = 0.95
matrix_rate = 0.03
vector_rate = 0.1
quintic_one = 3.4445
quintic_two = -4.775
quintic_three = 2.0315

def round_keep(values):
    return lax.optimization_barrier(values.astype(jnp.bfloat16))

def layer_norm(values):
    average = lax.optimization_barrier(jnp.mean(values, axis=-1, keepdims=True))
    centred = values - average
    variance = lax.optimization_barrier(jnp.mean(centred * centred, axis=-1, keepdims=True))
    inverse = lax.rsqrt(variance + norm_eps)
    return (centred * inverse, inverse)

def norm_back(gradient, standard, inverse, gain):
    scaled = gradient * gain
    first_mean = lax.optimization_barrier(jnp.mean(scaled, axis=-1, keepdims=True))
    second_mean = lax.optimization_barrier(jnp.mean(scaled * standard, axis=-1, keepdims=True))
    into = inverse * (scaled - first_mean - standard * second_mean)
    return (into, lax.optimization_barrier(jnp.sum(gradient * standard, axis=0)), lax.optimization_barrier(jnp.sum(gradient, axis=0)))

def gelu_value(pre_act):
    return pre_act * (0.5 * (1.0 + jax.scipy.special.erf(pre_act * 0.7071067811865476)))

def gelu_slope(pre_act):
    normal_cdf = 0.5 * (1.0 + jax.scipy.special.erf(pre_act * 0.7071067811865476))
    return normal_cdf + pre_act * jnp.exp(-0.5 * pre_act * pre_act) * 0.3989422804014327

def segment_tables(segment_ids):
    token_index = jnp.arange(segment_ids.shape[0], dtype=jnp.int32)
    allowed = (segment_ids[:, None] == segment_ids[None, :]) & (token_index[None, :] <= token_index[:, None])
    positions = lax.optimization_barrier(jnp.sum(allowed.astype(jnp.float32), axis=1)) - 1.0
    frequency = 10000.0 ** (-jnp.arange(0, ROT, 2, dtype=jnp.float32) / ROT)
    angles = positions[:, None] * frequency[None, :]
    cosine_table = jnp.concatenate([jnp.cos(angles), jnp.cos(angles)], axis=1)
    sine_table = jnp.concatenate([jnp.sin(angles), jnp.sin(angles)], axis=1)
    return (allowed, cosine_table, sine_table)

def rotate(field_rows, cosine_table, sine_table):
    half_dims = ROT // 2
    head_part = field_rows[..., :ROT]
    turned = jnp.concatenate([-head_part[..., half_dims:], head_part[..., :half_dims]], axis=-1)
    rotated = head_part * cosine_table[:, None, :] + turned * sine_table[:, None, :]
    return jnp.concatenate([rotated, field_rows[..., ROT:]], axis=-1)

def unrotate(grad_rows, cosine_table, sine_table):
    half_dims = ROT // 2
    head_part = grad_rows[..., :ROT]
    scaled = head_part * sine_table[:, None, :]
    back = jnp.concatenate([scaled[..., half_dims:], -scaled[..., :half_dims]], axis=-1)
    return jnp.concatenate([head_part * cosine_table[:, None, :] + back, grad_rows[..., ROT:]], axis=-1)

def orthogonalize(block):
    as_float = block.astype(jnp.float32)
    magnitude = jnp.sqrt(jnp.sum(as_float * as_float))
    iterate = round_keep(as_float / (magnitude + 1e-07))
    for iteration in range(NS_ITERS):
        gram_matrix = round_keep(jnp.dot(iterate.T, iterate, preferred_element_type=jnp.float32))
        squared = jnp.dot(gram_matrix, gram_matrix, preferred_element_type=jnp.float32)
        polynomial = (quintic_two * gram_matrix.astype(jnp.float32) + quintic_three * squared).astype(jnp.bfloat16)
        iterate = round_keep(quintic_one * iterate.astype(jnp.float32) + jnp.dot(iterate, polynomial, preferred_element_type=jnp.float32))
    return iterate

def to_blocks(attention_rows, output_rows, expand_rows, shrink_rows, local_heads):
    row_count, block_width = output_rows.shape
    query_like = attention_rows.reshape(row_count, local_heads, 3, block_width // local_heads).transpose(2, 0, 1, 3).reshape(3, row_count, block_width)
    expand_blocks = expand_rows.reshape(row_count, -1, block_width).transpose(1, 0, 2)
    shrink_blocks = shrink_rows.reshape(row_count, -1, block_width).transpose(1, 0, 2)
    return jnp.concatenate([query_like, output_rows[None], expand_blocks, shrink_blocks], axis=0)

def from_blocks(blocks, local_heads):
    block_count, row_count, block_width = blocks.shape
    ffn_blocks = (block_count - 4) // 2
    attention_rows = blocks[:3].reshape(3, row_count, local_heads, block_width // local_heads).transpose(1, 2, 0, 3).reshape(row_count, 3 * block_width)
    output_rows = blocks[3]
    expand_rows = blocks[4:4 + ffn_blocks].transpose(1, 0, 2).reshape(row_count, ffn_blocks * block_width)
    shrink_rows = blocks[4 + ffn_blocks:].transpose(1, 0, 2).reshape(row_count, ffn_blocks * block_width)
    return (attention_rows, output_rows, expand_rows, shrink_rows)

def add_terms(running, addend):
    return running + addend

def vector_step(param, gradient):
    return param - vector_rate * gradient * lax.rsqrt(jnp.mean(gradient * gradient) + 1e-06)

def reference(residual_in, out_cotangent, segments, first_gain, first_bias, second_gain, second_bias, attention_weight, attention_bias, output_weight, output_bias, expand_weight, expand_bias, shrink_weight, shrink_bias, attention_moment, output_moment, expand_moment, shrink_moment):
    attention_cast = attention_weight.astype(jnp.bfloat16)
    output_cast = output_weight.astype(jnp.bfloat16)
    expand_cast = expand_weight.astype(jnp.bfloat16)
    shrink_cast = shrink_weight.astype(jnp.bfloat16)
    head_scale = HEAD ** (-0.5)

    def one_block(carry, inputs):
        residual_rows, cot_rows, segment_ids = inputs
        allowed, cosine_table, sine_table = segment_tables(segment_ids)
        mask = allowed[None]
        standard, inverse = layer_norm(residual_rows)
        first_cast = (standard * first_gain + first_bias).astype(jnp.bfloat16)
        second_cast = (standard * second_gain + second_bias).astype(jnp.bfloat16)
        projected = jnp.dot(first_cast, attention_cast, preferred_element_type=jnp.float32) + attention_bias
        grouped = projected.reshape(TOK_DEV, HEADS, 3, HEAD)
        queries = rotate(grouped[:, :, 0], cosine_table, sine_table).astype(jnp.bfloat16)
        attn_keys = rotate(grouped[:, :, 1], cosine_table, sine_table).astype(jnp.bfloat16)
        attn_values = grouped[:, :, 2].astype(jnp.bfloat16)
        scores = jnp.einsum('thd,shd->hts', queries.astype(jnp.float32), attn_keys.astype(jnp.float32)) * head_scale
        exps = jnp.where(mask, jnp.exp(jnp.where(mask, scores, 0.0)), 0.0)
        totals = lax.optimization_barrier(jnp.sum(exps, axis=-1, keepdims=True))
        log_total = jnp.log(totals)
        probs = (exps / totals).astype(jnp.bfloat16)
        attended = jnp.einsum('hts,shd->thd', probs.astype(jnp.float32), attn_values.astype(jnp.float32)).reshape(TOK_DEV, D).astype(jnp.bfloat16)
        pre_act = jnp.dot(second_cast, expand_cast, preferred_element_type=jnp.float32) + expand_bias
        hidden = gelu_value(pre_act).astype(jnp.bfloat16)
        branch_sum = jnp.dot(attended, output_cast, preferred_element_type=jnp.float32) + jnp.dot(hidden, shrink_cast, preferred_element_type=jnp.float32)
        block_rows = residual_rows + branch_sum + output_bias + shrink_bias
        cot_cast = cot_rows.astype(jnp.bfloat16)
        pre_grad = jnp.dot(cot_cast, shrink_cast.T, preferred_element_type=jnp.float32) * gelu_slope(pre_act)
        pre_cast = pre_grad.astype(jnp.bfloat16)
        attended_grad = jnp.dot(cot_cast, output_cast.T, preferred_element_type=jnp.float32).astype(jnp.bfloat16)
        grad_heads = attended_grad.reshape(TOK_DEV, HEADS, HEAD).astype(jnp.float32)
        scores_again = jnp.einsum('thd,shd->hts', queries.astype(jnp.float32), attn_keys.astype(jnp.float32)) * head_scale
        probs_again = jnp.where(mask, jnp.exp(jnp.where(mask, scores_again - log_total, 0.0)), 0.0)
        prob_grad = jnp.einsum('thd,shd->hts', grad_heads, attn_values.astype(jnp.float32))
        row_delta = lax.optimization_barrier(jnp.sum(probs_again * prob_grad, axis=-1, keepdims=True))
        score_grad = (probs_again * (prob_grad - row_delta) * head_scale).astype(jnp.bfloat16).astype(jnp.float32)
        query_grad = unrotate(jnp.einsum('hts,shd->thd', score_grad, attn_keys.astype(jnp.float32)), cosine_table, sine_table)
        key_grad = unrotate(jnp.einsum('hts,thd->shd', score_grad, queries.astype(jnp.float32)), cosine_table, sine_table)
        value_grad = jnp.einsum('hts,thd->shd', probs_again.astype(jnp.bfloat16).astype(jnp.float32), grad_heads)
        projected_grad = jnp.stack([query_grad, key_grad, value_grad], axis=2).reshape(TOK_DEV, 3 * D)
        projected_cast = projected_grad.astype(jnp.bfloat16)
        first_grad = jnp.dot(projected_cast, attention_cast.T, preferred_element_type=jnp.float32)
        second_grad = jnp.dot(pre_cast, expand_cast.T, preferred_element_type=jnp.float32)
        first_into, first_gain_part, first_bias_part = norm_back(first_grad, standard, inverse, first_gain)
        second_into, second_gain_part, second_bias_part = norm_back(second_grad, standard, inverse, second_gain)
        residual_rows_grad = cot_rows + first_into + second_into
        weight_terms = (jnp.dot(first_cast.T, projected_cast, preferred_element_type=jnp.float32), jnp.dot(attended.T, cot_cast, preferred_element_type=jnp.float32), jnp.dot(second_cast.T, pre_cast, preferred_element_type=jnp.float32), jnp.dot(hidden.T, cot_cast, preferred_element_type=jnp.float32))
        vector_terms = (first_gain_part, first_bias_part, second_gain_part, second_bias_part, lax.optimization_barrier(jnp.sum(cot_rows, axis=0)), lax.optimization_barrier(jnp.sum(projected_grad, axis=0)), lax.optimization_barrier(jnp.sum(pre_grad, axis=0)))
        carry = jax.tree.map(add_terms, carry, (weight_terms, vector_terms))
        return (carry, (block_rows, residual_rows_grad))
    start = ((jnp.zeros((D, 3 * D), jnp.float32), jnp.zeros((D, D), jnp.float32), jnp.zeros((D, FF), jnp.float32), jnp.zeros((FF, D), jnp.float32)), (jnp.zeros((D,), jnp.float32), jnp.zeros((D,), jnp.float32), jnp.zeros((D,), jnp.float32), jnp.zeros((D,), jnp.float32), jnp.zeros((D,), jnp.float32), jnp.zeros((3 * D,), jnp.float32), jnp.zeros((FF,), jnp.float32)))
    inputs = (residual_in.reshape(N_DP, TOK_DEV, D), out_cotangent.reshape(N_DP, TOK_DEV, D), segments.reshape(N_DP, TOK_DEV))
    totals_all, row_outputs = lax.scan(one_block, start, inputs)
    weight_grads, vector_grads = totals_all
    block_out = row_outputs[0].reshape(TOKENS, D)
    residual_grad = row_outputs[1].reshape(TOKENS, D)
    attention_weight_grad, output_weight_grad, expand_weight_grad, shrink_weight_grad = weight_grads
    first_gain_grad, first_bias_grad, second_gain_grad, second_bias_grad, out_bias_grad, attention_bias_grad, expand_bias_grad = vector_grads
    moments = (attention_moment, output_moment, expand_moment, shrink_moment)
    moments_new = [momentum_rate * moment + gradient for moment, gradient in zip(moments, weight_grads)]
    nesterov = [round_keep(gradient + momentum_rate * moment) for moment, gradient in zip(moments_new, weight_grads)]
    block_width = D // N_TENSOR
    local_heads = HEADS // N_TENSOR
    ffn_half = FF // N_TENSOR
    halves = []
    for half_index in range(N_TENSOR):
        attention_rows = nesterov[0][:, half_index * 3 * block_width:(half_index + 1) * 3 * block_width]
        output_rows = nesterov[1][half_index * block_width:(half_index + 1) * block_width, :].T
        expand_rows = nesterov[2][:, half_index * ffn_half:(half_index + 1) * ffn_half]
        shrink_rows = nesterov[3][half_index * ffn_half:(half_index + 1) * ffn_half, :].T
        blocks = to_blocks(attention_rows, output_rows, expand_rows, shrink_rows, local_heads)
        results = lax.map(orthogonalize, blocks)
        halves.append(from_blocks(results, local_heads))
    update_attention = jnp.concatenate([piece[0] for piece in halves], axis=1).astype(jnp.float32)
    update_output = jnp.concatenate([piece[1].T for piece in halves], axis=0).astype(jnp.float32)
    update_expand = jnp.concatenate([piece[2] for piece in halves], axis=1).astype(jnp.float32)
    update_shrink = jnp.concatenate([piece[3].T for piece in halves], axis=0).astype(jnp.float32)
    step_scale = matrix_rate * 0.2 * math.sqrt(D)
    return (block_out, residual_grad, first_gain_grad, first_bias_grad, second_gain_grad, second_bias_grad, attention_weight_grad, attention_bias_grad, output_weight_grad, out_bias_grad, expand_weight_grad, expand_bias_grad, shrink_weight_grad, out_bias_grad, vector_step(first_gain, first_gain_grad), vector_step(first_bias, first_bias_grad), vector_step(second_gain, second_gain_grad), vector_step(second_bias, second_bias_grad), attention_weight - step_scale * update_attention, vector_step(attention_bias, attention_bias_grad), output_weight - step_scale * update_output, vector_step(output_bias, out_bias_grad), expand_weight - step_scale * update_expand, vector_step(expand_bias, expand_bias_grad), shrink_weight - step_scale * update_shrink, vector_step(shrink_bias, out_bias_grad), moments_new[0], moments_new[1], moments_new[2], moments_new[3])
```

```python
import math

import jax
import jax.numpy as jnp
from jax import lax
from jax.sharding import PartitionSpec as P

D = 768
HEAD = 64
ROT = 16
NS_ITERS = 4


norm_eps = 1e-05
momentum_rate = 0.95
matrix_rate = 0.03
vector_rate = 0.1
quintic_one = 3.4445
quintic_two = -4.775
quintic_three = 2.0315


def round_keep(values):
    return lax.optimization_barrier(values.astype(jnp.bfloat16))


def layer_norm(values):
    average = jnp.mean(values, axis=-1, keepdims=True)
    centred = values - average
    variance = jnp.mean(centred * centred, axis=-1, keepdims=True)
    inverse = lax.rsqrt(variance + norm_eps)
    return (centred * inverse, inverse)


def norm_back(gradient, standard, inverse, gain):
    scaled = gradient * gain
    first_mean = jnp.mean(scaled, axis=-1, keepdims=True)
    second_mean = jnp.mean(scaled * standard, axis=-1, keepdims=True)
    into = inverse * (scaled - first_mean - standard * second_mean)
    return (into, jnp.sum(gradient * standard, axis=0), jnp.sum(gradient, axis=0))


def gelu_value(pre_act):
    return pre_act * (0.5 * (1.0 + jax.scipy.special.erf(pre_act * 0.7071067811865476)))


def gelu_slope(pre_act):
    normal_cdf = 0.5 * (1.0 + jax.scipy.special.erf(pre_act * 0.7071067811865476))
    return normal_cdf + pre_act * jnp.exp(-0.5 * pre_act * pre_act) * 0.3989422804014327


def segment_tables(segment_ids):
    token_index = jnp.arange(segment_ids.shape[0], dtype=jnp.int32)
    allowed = (segment_ids[:, None] == segment_ids[None, :]) & (
        token_index[None, :] <= token_index[:, None]
    )
    positions = jnp.sum(allowed.astype(jnp.float32), axis=1) - 1.0
    frequency = 10000.0 ** (-jnp.arange(0, ROT, 2, dtype=jnp.float32) / ROT)
    angles = positions[:, None] * frequency[None, :]
    cosine_table = jnp.concatenate([jnp.cos(angles), jnp.cos(angles)], axis=1)
    sine_table = jnp.concatenate([jnp.sin(angles), jnp.sin(angles)], axis=1)
    return (allowed, cosine_table, sine_table)


def rotate(field_rows, cosine_table, sine_table):
    half_dims = ROT // 2
    head_part = field_rows[..., :ROT]
    turned = jnp.concatenate([-head_part[..., half_dims:], head_part[..., :half_dims]], axis=-1)
    rotated = head_part * cosine_table[:, None, :] + turned * sine_table[:, None, :]
    return jnp.concatenate([rotated, field_rows[..., ROT:]], axis=-1)


def unrotate(grad_rows, cosine_table, sine_table):
    half_dims = ROT // 2
    head_part = grad_rows[..., :ROT]
    scaled = head_part * sine_table[:, None, :]
    back = jnp.concatenate([scaled[..., half_dims:], -scaled[..., :half_dims]], axis=-1)
    return jnp.concatenate(
        [head_part * cosine_table[:, None, :] + back, grad_rows[..., ROT:]], axis=-1
    )


def orthogonalize(block):
    as_float = block.astype(jnp.float32)
    magnitude = jnp.sqrt(jnp.sum(as_float * as_float))
    iterate = round_keep(as_float / (magnitude + 1e-07))
    for iteration in range(NS_ITERS):
        gram_matrix = round_keep(
            lax.dot_general(
                iterate, iterate, (((0,), (0,)), ((), ())), preferred_element_type=jnp.float32
            )
        )
        squared = jnp.dot(gram_matrix, gram_matrix, preferred_element_type=jnp.float32)
        polynomial = (
            quintic_two * gram_matrix.astype(jnp.float32) + quintic_three * squared
        ).astype(jnp.bfloat16)
        iterate = round_keep(
            quintic_one * iterate.astype(jnp.float32)
            + jnp.dot(iterate, polynomial, preferred_element_type=jnp.float32)
        )
    return iterate


def to_blocks(attention_rows, output_rows, expand_rows, shrink_rows, local_heads):
    row_count, block_width = output_rows.shape
    query_like = (
        attention_rows.reshape(row_count, local_heads, 3, block_width // local_heads)
        .transpose(2, 0, 1, 3)
        .reshape(3, row_count, block_width)
    )
    expand_blocks = expand_rows.reshape(row_count, -1, block_width).transpose(1, 0, 2)
    shrink_blocks = shrink_rows.reshape(row_count, -1, block_width).transpose(1, 0, 2)
    return jnp.concatenate([query_like, output_rows[None], expand_blocks, shrink_blocks], axis=0)


def from_blocks(blocks, local_heads):
    block_count, row_count, block_width = blocks.shape
    ffn_blocks = (block_count - 4) // 2
    attention_rows = (
        blocks[:3]
        .reshape(3, row_count, local_heads, block_width // local_heads)
        .transpose(1, 2, 0, 3)
        .reshape(row_count, 3 * block_width)
    )
    output_rows = blocks[3]
    expand_rows = (
        blocks[4 : 4 + ffn_blocks].transpose(1, 0, 2).reshape(row_count, ffn_blocks * block_width)
    )
    shrink_rows = (
        blocks[4 + ffn_blocks :].transpose(1, 0, 2).reshape(row_count, ffn_blocks * block_width)
    )
    return (attention_rows, output_rows, expand_rows, shrink_rows)


def vector_step(param, gradient, whole_gradient):
    return param - vector_rate * gradient * lax.rsqrt(
        jnp.mean(whole_gradient * whole_gradient) + 1e-06
    )


def exchange(values, bit):
    count = lax.axis_size("dp")
    return lax.ppermute(values, "dp", [(i, i ^ (1 << bit)) for i in range(count)])


def swap_cores(values):
    return lax.ppermute(values, "tensor", [(0, 1), (1, 0)])


def bit_orders():
    bits = (lax.axis_size("dp") - 1).bit_length()
    rising = list(range(bits))
    swapped = rising[1::-1] + rising[2:]
    return (rising, swapped)


def own_bit(bit):
    return (lax.axis_index("dp") >> bit) & 1


def gather_rows(shard, order):
    values, held = (shard, [])
    for bit in reversed(order):
        other = exchange(values, bit)
        low = own_bit(bit) == 0
        place = sum(1 for have in held if have > bit)
        values = jnp.stack(
            [jnp.where(low, values, other), jnp.where(low, other, values)], axis=place
        )
        held.append(bit)
    return values.reshape(-1, shard.shape[1])


def scatter_sum(partial, order):
    count = lax.axis_size("dp")
    rows, columns = partial.shape
    values = partial.reshape([2] * len(order) + [rows // count, columns])
    left = sorted(order, reverse=True)
    for bit in order:
        axis = left.index(bit)
        mine = own_bit(bit)
        send = lax.dynamic_index_in_dim(values, 1 - mine, axis, keepdims=False)
        keep = lax.dynamic_index_in_dim(values, mine, axis, keepdims=False)
        values = keep + exchange(send.astype(jnp.bfloat16), bit).astype(jnp.float32)
        left.remove(bit)
    return values


def join_cores(values):
    other = swap_cores(values)
    first = lax.axis_index("tensor") == 0
    return jnp.concatenate(
        [jnp.where(first, values, other), jnp.where(first, other, values)], axis=0
    )


def split_cores(values):
    half = values.shape[0] // 2
    side = lax.axis_index("tensor")
    send = lax.dynamic_slice_in_dim(values, (1 - side) * half, half)
    keep = lax.dynamic_slice_in_dim(values, side * half, half)
    return keep + swap_cores(send)


def shards(
    residual_in,
    out_cotangent,
    segments,
    first_gain,
    first_bias,
    second_gain,
    second_bias,
    attention_weight,
    attention_bias,
    output_weight,
    output_bias,
    expand_weight,
    expand_bias,
    shrink_weight,
    shrink_bias,
    attention_moment,
    output_moment,
    expand_moment,
    shrink_moment,
):
    row_count = residual_in.shape[1]
    block_width = output_weight.shape[0]
    local_heads = block_width // HEAD
    ffn_half = expand_weight.shape[1]
    token_count = segments.shape[0]
    head_scale = HEAD ** (-0.5)
    rising, swapped = bit_orders()
    half_width = 2 * block_width

    def gather_pair(rows):
        middle = rows.shape[1] // 2
        return (gather_rows(rows[:, :middle], rising), gather_rows(rows[:, middle:], swapped))

    attention_rows = jnp.concatenate([attention_weight, output_weight.T], axis=1)
    mixed_cast = gather_pair(attention_rows.astype(jnp.bfloat16))
    attention_cast = jnp.concatenate([mixed_cast[0], mixed_cast[1][:, :block_width]], axis=1)
    output_turned = mixed_cast[1][:, block_width:]
    expand_cast = jnp.concatenate(gather_pair(expand_weight.astype(jnp.bfloat16)), axis=1)
    shrink_turned = jnp.concatenate(gather_pair(shrink_weight.T.astype(jnp.bfloat16)), axis=1)
    standard, inverse = layer_norm(residual_in)
    first_normed = (standard * first_gain + first_bias).astype(jnp.bfloat16)
    second_normed = (standard * second_gain + second_bias).astype(jnp.bfloat16)
    joined = join_cores(
        jnp.concatenate([first_normed, second_normed, out_cotangent.astype(jnp.bfloat16)], axis=1)
    )
    first_cast, second_cast, cot_cast = (
        joined[:, :row_count],
        joined[:, row_count : 2 * row_count],
        joined[:, 2 * row_count :],
    )
    allowed, cosine_table, sine_table = segment_tables(segments)
    mask = allowed[None]
    projected = (
        jnp.dot(first_cast, attention_cast, preferred_element_type=jnp.float32) + attention_bias
    )
    grouped = projected.reshape(token_count, local_heads, 3, HEAD)
    queries = rotate(grouped[:, :, 0], cosine_table, sine_table).astype(jnp.bfloat16)
    attn_keys = rotate(grouped[:, :, 1], cosine_table, sine_table).astype(jnp.bfloat16)
    attn_values = grouped[:, :, 2].astype(jnp.bfloat16)
    scores = (
        jnp.einsum("thd,shd->hts", queries, attn_keys, preferred_element_type=jnp.float32)
        * head_scale
    )
    exps = jnp.where(mask, jnp.exp(jnp.where(mask, scores, 0.0)), 0.0)
    totals = jnp.sum(exps, axis=-1, keepdims=True)
    log_total = jnp.log(totals)
    probs = (exps / totals).astype(jnp.bfloat16)
    attended = (
        jnp.einsum("hts,shd->thd", probs, attn_values, preferred_element_type=jnp.float32)
        .reshape(token_count, block_width)
        .astype(jnp.bfloat16)
    )
    pre_act = jnp.dot(second_cast, expand_cast, preferred_element_type=jnp.float32) + expand_bias
    hidden = gelu_value(pre_act).astype(jnp.bfloat16)
    turned = (((1,), (1,)), ((), ()))
    partial_sum = lax.dot_general(
        attended, output_turned, turned, preferred_element_type=jnp.float32
    ) + lax.dot_general(hidden, shrink_turned, turned, preferred_element_type=jnp.float32)
    branch_sum = split_cores(partial_sum)
    block_out = residual_in + branch_sum + output_bias + shrink_bias
    pre_grad = jnp.dot(cot_cast, shrink_turned, preferred_element_type=jnp.float32) * gelu_slope(
        pre_act
    )
    pre_cast = pre_grad.astype(jnp.bfloat16)
    attended_grad = jnp.dot(cot_cast, output_turned, preferred_element_type=jnp.float32).astype(
        jnp.bfloat16
    )
    grad_heads = attended_grad.reshape(token_count, local_heads, HEAD)
    scores_again = (
        jnp.einsum("thd,shd->hts", queries, attn_keys, preferred_element_type=jnp.float32)
        * head_scale
    )
    probs_again = jnp.where(mask, jnp.exp(jnp.where(mask, scores_again - log_total, 0.0)), 0.0)
    prob_grad = jnp.einsum(
        "thd,shd->hts", grad_heads, attn_values, preferred_element_type=jnp.float32
    )
    row_delta = jnp.sum(probs_again * prob_grad, axis=-1, keepdims=True)
    score_grad = (probs_again * (prob_grad - row_delta) * head_scale).astype(jnp.bfloat16)
    query_grad = unrotate(
        jnp.einsum("hts,shd->thd", score_grad, attn_keys, preferred_element_type=jnp.float32),
        cosine_table,
        sine_table,
    )
    key_grad = unrotate(
        jnp.einsum("hts,thd->shd", score_grad, queries, preferred_element_type=jnp.float32),
        cosine_table,
        sine_table,
    )
    value_grad = jnp.einsum(
        "hts,thd->shd",
        probs_again.astype(jnp.bfloat16),
        grad_heads,
        preferred_element_type=jnp.float32,
    )
    projected_grad = jnp.stack([query_grad, key_grad, value_grad], axis=2).reshape(
        token_count, 3 * block_width
    )
    projected_cast = projected_grad.astype(jnp.bfloat16)
    first_part = jnp.dot(projected_cast, attention_cast.T, preferred_element_type=jnp.float32)
    second_part = jnp.dot(pre_cast, expand_cast.T, preferred_element_type=jnp.float32)
    first_grad, second_grad = (split_cores(first_part), split_cores(second_part))
    first_into, first_gain_part, first_bias_part = norm_back(
        first_grad, standard, inverse, first_gain
    )
    second_into, second_gain_part, second_bias_part = norm_back(
        second_grad, standard, inverse, second_gain
    )
    residual_grad = out_cotangent + first_into + second_into
    contract = (((0,), (0,)), ((), ()))

    def columns_grad(left, right):
        return lax.dot_general(left, right, contract, preferred_element_type=jnp.float32)

    def scatter_pair(left, right):
        middle = right.shape[1] // 2
        return jnp.concatenate(
            [
                scatter_sum(columns_grad(left, right[:, :middle]), rising),
                scatter_sum(columns_grad(left, right[:, middle:]), swapped),
            ],
            axis=1,
        )

    shrink_rows_grad = scatter_pair(cot_cast, hidden)
    expand_weight_grad = scatter_pair(second_cast, pre_cast)
    attention_first = scatter_sum(columns_grad(first_cast, projected_cast[:, :half_width]), rising)
    attention_second = scatter_sum(
        jnp.concatenate(
            [
                columns_grad(first_cast, projected_cast[:, half_width:]),
                columns_grad(cot_cast, attended),
            ],
            axis=1,
        ),
        swapped,
    )
    attention_weight_grad = jnp.concatenate(
        [attention_first, attention_second[:, :block_width]], axis=1
    )
    output_rows_grad = attention_second[:, block_width:]
    vectors = jnp.concatenate(
        [
            first_gain_part,
            first_bias_part,
            second_gain_part,
            second_bias_part,
            jnp.sum(out_cotangent, axis=0),
            jnp.sum(projected_grad, axis=0),
            jnp.sum(pre_grad, axis=0),
        ]
    ).reshape(-1, 128)
    for bit in rising:
        vectors = vectors + exchange(vectors, bit)
    other_vectors = swap_cores(vectors).reshape(-1)
    vectors = vectors.reshape(-1)
    shared = 5 * row_count
    vector_sums = (vectors[:shared] + other_vectors[:shared]).reshape(5, row_count)
    attention_end = shared + 3 * block_width
    attention_bias_grad = vectors[shared:attention_end]
    expand_bias_grad = vectors[attention_end:]
    attention_bias_sum = jnp.stack([attention_bias_grad, other_vectors[shared:attention_end]])
    expand_bias_sum = jnp.stack([expand_bias_grad, other_vectors[attention_end:]])
    moment_rows = (attention_moment, output_moment.T, expand_moment, shrink_moment.T)
    grad_rows = (attention_weight_grad, output_rows_grad, expand_weight_grad, shrink_rows_grad)
    moments_new = [
        momentum_rate * moment + gradient for moment, gradient in zip(moment_rows, grad_rows)
    ]
    nesterov = [
        (gradient + momentum_rate * moment).astype(jnp.bfloat16)
        for moment, gradient in zip(moments_new, grad_rows)
    ]
    stacked = to_blocks(nesterov[0], nesterov[1], nesterov[2], nesterov[3], local_heads)
    block_count = stacked.shape[0]
    padded = jnp.pad(stacked, ((0, lax.axis_size("dp") - block_count), (0, 0), (0, 0)))
    chosen = lax.all_to_all(padded, "dp", split_axis=0, concat_axis=1, tiled=True)[0]
    result = orthogonalize(chosen)
    returned = lax.all_to_all(result[None], "dp", split_axis=1, concat_axis=0, tiled=True)
    updates = returned[:block_count]
    update_attention, update_output, update_expand, update_shrink = from_blocks(
        updates, local_heads
    )
    step_scale = matrix_rate * 0.2 * math.sqrt(D)
    attention_weight_new = attention_weight - step_scale * update_attention.astype(jnp.float32)
    output_weight_new = output_weight - step_scale * update_output.T.astype(jnp.float32)
    expand_weight_new = expand_weight - step_scale * update_expand.astype(jnp.float32)
    shrink_weight_new = shrink_weight - step_scale * update_shrink.T.astype(jnp.float32)
    out_bias_grad = vector_sums[4]
    return (
        block_out,
        residual_grad,
        vector_sums[0],
        vector_sums[1],
        vector_sums[2],
        vector_sums[3],
        attention_weight_grad,
        attention_bias_grad,
        output_rows_grad.T,
        out_bias_grad,
        expand_weight_grad,
        expand_bias_grad,
        shrink_rows_grad.T,
        out_bias_grad,
        vector_step(first_gain, vector_sums[0], vector_sums[0]),
        vector_step(first_bias, vector_sums[1], vector_sums[1]),
        vector_step(second_gain, vector_sums[2], vector_sums[2]),
        vector_step(second_bias, vector_sums[3], vector_sums[3]),
        attention_weight_new,
        vector_step(attention_bias, attention_bias_grad, attention_bias_sum),
        output_weight_new,
        vector_step(output_bias, out_bias_grad, out_bias_grad),
        expand_weight_new,
        vector_step(expand_bias, expand_bias_grad, expand_bias_sum),
        shrink_weight_new,
        vector_step(shrink_bias, out_bias_grad, out_bias_grad),
        moments_new[0],
        moments_new[1].T,
        moments_new[2],
        moments_new[3].T,
    )


def solution(mesh):
    return jax.shard_map(
        shards,
        mesh=mesh,
        in_specs=(
            P(("dp", "tensor"), None),
            P(("dp", "tensor"), None),
            P("dp"),
            P(),
            P(),
            P(),
            P(),
            P("dp", "tensor"),
            P("tensor"),
            P("tensor", "dp"),
            P(),
            P("dp", "tensor"),
            P("tensor"),
            P("tensor", "dp"),
            P(),
            P("dp", "tensor"),
            P("tensor", "dp"),
            P("dp", "tensor"),
            P("tensor", "dp"),
        ),
        out_specs=(
            P(("dp", "tensor"), None),
            P(("dp", "tensor"), None),
            P(),
            P(),
            P(),
            P(),
            P("dp", "tensor"),
            P("tensor"),
            P("tensor", "dp"),
            P(),
            P("dp", "tensor"),
            P("tensor"),
            P("tensor", "dp"),
            P(),
            P(),
            P(),
            P(),
            P(),
            P("dp", "tensor"),
            P("tensor"),
            P("tensor", "dp"),
            P(),
            P("dp", "tensor"),
            P("tensor"),
            P("tensor", "dp"),
            P(),
            P("dp", "tensor"),
            P("tensor", "dp"),
            P("dp", "tensor"),
            P("tensor", "dp"),
        ),
        check_vma=False,
    )
```

```python
import math

import jax
import jax.numpy as jnp
from jax import lax
from jax.sharding import PartitionSpec as P

D = 768
HEAD = 64
ROT = 16
NS_ITERS = 4


norm_eps = 1e-05
momentum_rate = 0.95
matrix_rate = 0.03
vector_rate = 0.1
quintic_one = 3.4445
quintic_two = -4.775
quintic_three = 2.0315


def round_keep(values):
    return lax.optimization_barrier(values.astype(jnp.bfloat16))


def layer_norm(values):
    average = jnp.mean(values, axis=-1, keepdims=True)
    centred = values - average
    variance = jnp.mean(centred * centred, axis=-1, keepdims=True)
    inverse = lax.rsqrt(variance + norm_eps)
    return (centred * inverse, inverse)


def norm_back(gradient, standard, inverse, gain):
    scaled = gradient * gain
    first_mean = jnp.mean(scaled, axis=-1, keepdims=True)
    second_mean = jnp.mean(scaled * standard, axis=-1, keepdims=True)
    into = inverse * (scaled - first_mean - standard * second_mean)
    return (into, jnp.sum(gradient * standard, axis=0), jnp.sum(gradient, axis=0))


def gelu_value(pre_act):
    return pre_act * (0.5 * (1.0 + jax.scipy.special.erf(pre_act * 0.7071067811865476)))


def gelu_slope(pre_act):
    normal_cdf = 0.5 * (1.0 + jax.scipy.special.erf(pre_act * 0.7071067811865476))
    return normal_cdf + pre_act * jnp.exp(-0.5 * pre_act * pre_act) * 0.3989422804014327


def segment_tables(segment_ids):
    token_index = jnp.arange(segment_ids.shape[0], dtype=jnp.int32)
    allowed = (segment_ids[:, None] == segment_ids[None, :]) & (
        token_index[None, :] <= token_index[:, None]
    )
    positions = jnp.sum(allowed.astype(jnp.float32), axis=1) - 1.0
    frequency = 10000.0 ** (-jnp.arange(0, ROT, 2, dtype=jnp.float32) / ROT)
    angles = positions[:, None] * frequency[None, :]
    cosine_table = jnp.concatenate([jnp.cos(angles), jnp.cos(angles)], axis=1)
    sine_table = jnp.concatenate([jnp.sin(angles), jnp.sin(angles)], axis=1)
    return (allowed, cosine_table, sine_table)


def rotate(field_rows, cosine_table, sine_table):
    half_dims = ROT // 2
    head_part = field_rows[..., :ROT]
    turned = jnp.concatenate([-head_part[..., half_dims:], head_part[..., :half_dims]], axis=-1)
    rotated = head_part * cosine_table[:, None, :] + turned * sine_table[:, None, :]
    return jnp.concatenate([rotated, field_rows[..., ROT:]], axis=-1)


def unrotate(grad_rows, cosine_table, sine_table):
    half_dims = ROT // 2
    head_part = grad_rows[..., :ROT]
    scaled = head_part * sine_table[:, None, :]
    back = jnp.concatenate([scaled[..., half_dims:], -scaled[..., :half_dims]], axis=-1)
    return jnp.concatenate(
        [head_part * cosine_table[:, None, :] + back, grad_rows[..., ROT:]], axis=-1
    )


def orthogonalize(block):
    as_float = block.astype(jnp.float32)
    magnitude = jnp.sqrt(jnp.sum(as_float * as_float))
    iterate = round_keep(as_float / (magnitude + 1e-07))
    for iteration in range(NS_ITERS):
        gram_matrix = round_keep(
            lax.dot_general(
                iterate, iterate, (((0,), (0,)), ((), ())), preferred_element_type=jnp.float32
            )
        )
        squared = jnp.dot(gram_matrix, gram_matrix, preferred_element_type=jnp.float32)
        polynomial = (
            quintic_two * gram_matrix.astype(jnp.float32) + quintic_three * squared
        ).astype(jnp.bfloat16)
        iterate = round_keep(
            quintic_one * iterate.astype(jnp.float32)
            + jnp.dot(iterate, polynomial, preferred_element_type=jnp.float32)
        )
    return iterate


def to_blocks(attention_rows, output_rows, expand_rows, shrink_rows, local_heads):
    row_count, block_width = output_rows.shape
    query_like = (
        attention_rows.reshape(row_count, local_heads, 3, block_width // local_heads)
        .transpose(2, 0, 1, 3)
        .reshape(3, row_count, block_width)
    )
    expand_blocks = expand_rows.reshape(row_count, -1, block_width).transpose(1, 0, 2)
    shrink_blocks = shrink_rows.reshape(row_count, -1, block_width).transpose(1, 0, 2)
    return jnp.concatenate([query_like, output_rows[None], expand_blocks, shrink_blocks], axis=0)


def from_blocks(blocks, local_heads):
    block_count, row_count, block_width = blocks.shape
    ffn_blocks = (block_count - 4) // 2
    attention_rows = (
        blocks[:3]
        .reshape(3, row_count, local_heads, block_width // local_heads)
        .transpose(1, 2, 0, 3)
        .reshape(row_count, 3 * block_width)
    )
    output_rows = blocks[3]
    expand_rows = (
        blocks[4 : 4 + ffn_blocks].transpose(1, 0, 2).reshape(row_count, ffn_blocks * block_width)
    )
    shrink_rows = (
        blocks[4 + ffn_blocks :].transpose(1, 0, 2).reshape(row_count, ffn_blocks * block_width)
    )
    return (attention_rows, output_rows, expand_rows, shrink_rows)


def vector_step(param, gradient, whole_gradient):
    return param - vector_rate * gradient * lax.rsqrt(
        jnp.mean(whole_gradient * whole_gradient) + 1e-06
    )


def exchange(values, bit):
    count = lax.axis_size("dp")
    return lax.ppermute(values, "dp", [(i, i ^ (1 << bit)) for i in range(count)])


def swap_cores(values):
    return lax.ppermute(values, "tensor", [(0, 1), (1, 0)])


def bit_orders():
    bits = (lax.axis_size("dp") - 1).bit_length()
    rising = list(range(bits))
    swapped = rising[1::-1] + rising[2:]
    return (rising, swapped)


def own_bit(bit):
    return (lax.axis_index("dp") >> bit) & 1


def widen(values, held, bit):
    other = exchange(values, bit)
    low = own_bit(bit) == 0
    place = sum(1 for have in held if have > bit)
    return jnp.stack(
        [jnp.where(low, values, other), jnp.where(low, other, values)], axis=place
    )


def gather_pair(first, second):
    rising, swapped = bit_orders()
    width = first.shape[1]
    values, held = (jnp.concatenate([first, second], axis=1), [])
    for bit in reversed(rising[2:]):
        values = widen(values, held, bit)
        held.append(bit)
    gathered = []
    for part, order in ((values[..., :width], rising[:2]), (values[..., width:], swapped[:2])):
        have = list(held)
        for bit in reversed(order):
            part = widen(part, have, bit)
            have.append(bit)
        gathered.append(part.reshape(-1, part.shape[-1]))
    return gathered


def halve(values, left, bit):
    axis = left.index(bit)
    mine = own_bit(bit)
    send = lax.dynamic_index_in_dim(values, 1 - mine, axis, keepdims=False)
    keep = lax.dynamic_index_in_dim(values, mine, axis, keepdims=False)
    return keep + exchange(send.astype(jnp.bfloat16), bit).astype(jnp.float32)


def scatter_pair(first, second):
    rising, swapped = bit_orders()
    count = lax.axis_size("dp")
    halved = []
    for partial, order in ((first, rising[:2]), (second, swapped[:2])):
        rows, columns = partial.shape
        values = partial.reshape([2] * len(rising) + [rows // count, columns])
        left = rising[::-1]
        for bit in order:
            values = halve(values, left, bit)
            left.remove(bit)
        halved.append(values)
    values = jnp.concatenate(halved, axis=-1)
    left = rising[:1:-1]
    for bit in rising[2:]:
        values = halve(values, left, bit)
        left.remove(bit)
    return (values[:, : first.shape[1]], values[:, first.shape[1] :])


def join_cores(values):
    other = swap_cores(values)
    first = lax.axis_index("tensor") == 0
    return jnp.concatenate(
        [jnp.where(first, values, other), jnp.where(first, other, values)], axis=0
    )


def split_cores(values):
    half = values.shape[0] // 2
    side = lax.axis_index("tensor")
    send = lax.dynamic_slice_in_dim(values, (1 - side) * half, half)
    keep = lax.dynamic_slice_in_dim(values, side * half, half)
    return keep + swap_cores(send)


def shards(
    residual_in,
    out_cotangent,
    segments,
    first_gain,
    first_bias,
    second_gain,
    second_bias,
    attention_weight,
    attention_bias,
    output_weight,
    output_bias,
    expand_weight,
    expand_bias,
    shrink_weight,
    shrink_bias,
    attention_moment,
    output_moment,
    expand_moment,
    shrink_moment,
):
    row_count = residual_in.shape[1]
    block_width = output_weight.shape[0]
    local_heads = block_width // HEAD
    ffn_half = expand_weight.shape[1]
    token_count = segments.shape[0]
    head_scale = HEAD ** (-0.5)
    half_width = 2 * block_width
    attention_rows = attention_weight.astype(jnp.bfloat16)
    mixed_cast = gather_pair(
        attention_rows[:, :half_width],
        jnp.concatenate(
            [attention_rows[:, half_width:], output_weight.T.astype(jnp.bfloat16)], axis=1
        ),
    )
    attention_cast = jnp.concatenate([mixed_cast[0], mixed_cast[1][:, :block_width]], axis=1)
    output_turned = mixed_cast[1][:, block_width:]
    expand_cast, shrink_turned = gather_pair(
        expand_weight.astype(jnp.bfloat16), shrink_weight.T.astype(jnp.bfloat16)
    )
    standard, inverse = layer_norm(residual_in)
    first_normed = (standard * first_gain + first_bias).astype(jnp.bfloat16)
    second_normed = (standard * second_gain + second_bias).astype(jnp.bfloat16)
    joined = join_cores(
        jnp.concatenate([first_normed, second_normed, out_cotangent.astype(jnp.bfloat16)], axis=1)
    )
    first_cast, second_cast, cot_cast = (
        joined[:, :row_count],
        joined[:, row_count : 2 * row_count],
        joined[:, 2 * row_count :],
    )
    allowed, cosine_table, sine_table = segment_tables(segments)
    mask = allowed[None]
    projected = (
        jnp.dot(first_cast, attention_cast, preferred_element_type=jnp.float32) + attention_bias
    )
    grouped = projected.reshape(token_count, local_heads, 3, HEAD)
    queries = rotate(grouped[:, :, 0], cosine_table, sine_table).astype(jnp.bfloat16)
    attn_keys = rotate(grouped[:, :, 1], cosine_table, sine_table).astype(jnp.bfloat16)
    attn_values = grouped[:, :, 2].astype(jnp.bfloat16)
    scores = (
        jnp.einsum("thd,shd->hts", queries, attn_keys, preferred_element_type=jnp.float32)
        * head_scale
    )
    exps = jnp.where(mask, jnp.exp(jnp.where(mask, scores, 0.0)), 0.0)
    totals = jnp.sum(exps, axis=-1, keepdims=True)
    log_total = jnp.log(totals)
    probs = (exps / totals).astype(jnp.bfloat16)
    attended = (
        jnp.einsum("hts,shd->thd", probs, attn_values, preferred_element_type=jnp.float32)
        .reshape(token_count, block_width)
        .astype(jnp.bfloat16)
    )
    pre_act = jnp.dot(second_cast, expand_cast, preferred_element_type=jnp.float32) + expand_bias
    hidden = gelu_value(pre_act).astype(jnp.bfloat16)
    turned = (((1,), (1,)), ((), ()))
    partial_sum = lax.dot_general(
        attended, output_turned, turned, preferred_element_type=jnp.float32
    ) + lax.dot_general(hidden, shrink_turned, turned, preferred_element_type=jnp.float32)
    branch_sum = split_cores(partial_sum)
    block_out = residual_in + branch_sum + output_bias + shrink_bias
    pre_grad = jnp.dot(cot_cast, shrink_turned, preferred_element_type=jnp.float32) * gelu_slope(
        pre_act
    )
    pre_cast = pre_grad.astype(jnp.bfloat16)
    attended_grad = jnp.dot(cot_cast, output_turned, preferred_element_type=jnp.float32).astype(
        jnp.bfloat16
    )
    grad_heads = attended_grad.reshape(token_count, local_heads, HEAD)
    scores_again = (
        jnp.einsum("thd,shd->hts", queries, attn_keys, preferred_element_type=jnp.float32)
        * head_scale
    )
    probs_again = jnp.where(mask, jnp.exp(jnp.where(mask, scores_again - log_total, 0.0)), 0.0)
    prob_grad = jnp.einsum(
        "thd,shd->hts", grad_heads, attn_values, preferred_element_type=jnp.float32
    )
    row_delta = jnp.sum(probs_again * prob_grad, axis=-1, keepdims=True)
    score_grad = (probs_again * (prob_grad - row_delta) * head_scale).astype(jnp.bfloat16)
    query_grad = unrotate(
        jnp.einsum("hts,shd->thd", score_grad, attn_keys, preferred_element_type=jnp.float32),
        cosine_table,
        sine_table,
    )
    key_grad = unrotate(
        jnp.einsum("hts,thd->shd", score_grad, queries, preferred_element_type=jnp.float32),
        cosine_table,
        sine_table,
    )
    value_grad = jnp.einsum(
        "hts,thd->shd",
        probs_again.astype(jnp.bfloat16),
        grad_heads,
        preferred_element_type=jnp.float32,
    )
    projected_grad = jnp.stack([query_grad, key_grad, value_grad], axis=2).reshape(
        token_count, 3 * block_width
    )
    projected_cast = projected_grad.astype(jnp.bfloat16)
    first_part = jnp.dot(projected_cast, attention_cast.T, preferred_element_type=jnp.float32)
    second_part = jnp.dot(pre_cast, expand_cast.T, preferred_element_type=jnp.float32)
    first_grad, second_grad = (split_cores(first_part), split_cores(second_part))
    first_into, first_gain_part, first_bias_part = norm_back(
        first_grad, standard, inverse, first_gain
    )
    second_into, second_gain_part, second_bias_part = norm_back(
        second_grad, standard, inverse, second_gain
    )
    residual_grad = out_cotangent + first_into + second_into
    contract = (((0,), (0,)), ((), ()))

    def columns_grad(left, right):
        return lax.dot_general(left, right, contract, preferred_element_type=jnp.float32)

    shrink_rows_grad, expand_weight_grad = scatter_pair(
        columns_grad(cot_cast, hidden), columns_grad(second_cast, pre_cast)
    )
    attention_first, attention_second = scatter_pair(
        columns_grad(first_cast, projected_cast[:, :half_width]),
        jnp.concatenate(
            [
                columns_grad(first_cast, projected_cast[:, half_width:]),
                columns_grad(cot_cast, attended),
            ],
            axis=1,
        ),
    )
    attention_weight_grad = jnp.concatenate(
        [attention_first, attention_second[:, :block_width]], axis=1
    )
    output_rows_grad = attention_second[:, block_width:]
    vectors = jnp.concatenate(
        [
            first_gain_part,
            first_bias_part,
            second_gain_part,
            second_bias_part,
            jnp.sum(out_cotangent, axis=0),
            jnp.sum(projected_grad, axis=0),
            jnp.sum(pre_grad, axis=0),
        ]
    ).reshape(-1, 128)
    for bit in bit_orders()[0]:
        vectors = vectors + exchange(vectors, bit)
    other_vectors = swap_cores(vectors).reshape(-1)
    vectors = vectors.reshape(-1)
    shared = 5 * row_count
    vector_sums = (vectors[:shared] + other_vectors[:shared]).reshape(5, row_count)
    attention_end = shared + 3 * block_width
    attention_bias_grad = vectors[shared:attention_end]
    expand_bias_grad = vectors[attention_end:]
    attention_bias_sum = jnp.stack([attention_bias_grad, other_vectors[shared:attention_end]])
    expand_bias_sum = jnp.stack([expand_bias_grad, other_vectors[attention_end:]])
    moment_rows = (attention_moment, output_moment.T, expand_moment, shrink_moment.T)
    grad_rows = (attention_weight_grad, output_rows_grad, expand_weight_grad, shrink_rows_grad)
    moments_new = [
        momentum_rate * moment + gradient for moment, gradient in zip(moment_rows, grad_rows)
    ]
    nesterov = [
        (gradient + momentum_rate * moment).astype(jnp.bfloat16)
        for moment, gradient in zip(moments_new, grad_rows)
    ]
    stacked = to_blocks(nesterov[0], nesterov[1], nesterov[2], nesterov[3], local_heads)
    block_count = stacked.shape[0]
    padded = jnp.pad(stacked, ((0, lax.axis_size("dp") - block_count), (0, 0), (0, 0)))
    chosen = lax.all_to_all(padded, "dp", split_axis=0, concat_axis=1, tiled=True)[0]
    result = orthogonalize(chosen)
    returned = lax.all_to_all(result[None], "dp", split_axis=1, concat_axis=0, tiled=True)
    updates = returned[:block_count]
    update_attention, update_output, update_expand, update_shrink = from_blocks(
        updates, local_heads
    )
    step_scale = matrix_rate * 0.2 * math.sqrt(D)
    attention_weight_new = attention_weight - step_scale * update_attention.astype(jnp.float32)
    output_weight_new = output_weight - step_scale * update_output.T.astype(jnp.float32)
    expand_weight_new = expand_weight - step_scale * update_expand.astype(jnp.float32)
    shrink_weight_new = shrink_weight - step_scale * update_shrink.T.astype(jnp.float32)
    out_bias_grad = vector_sums[4]
    return (
        block_out,
        residual_grad,
        vector_sums[0],
        vector_sums[1],
        vector_sums[2],
        vector_sums[3],
        attention_weight_grad,
        attention_bias_grad,
        output_rows_grad.T,
        out_bias_grad,
        expand_weight_grad,
        expand_bias_grad,
        shrink_rows_grad.T,
        out_bias_grad,
        vector_step(first_gain, vector_sums[0], vector_sums[0]),
        vector_step(first_bias, vector_sums[1], vector_sums[1]),
        vector_step(second_gain, vector_sums[2], vector_sums[2]),
        vector_step(second_bias, vector_sums[3], vector_sums[3]),
        attention_weight_new,
        vector_step(attention_bias, attention_bias_grad, attention_bias_sum),
        output_weight_new,
        vector_step(output_bias, out_bias_grad, out_bias_grad),
        expand_weight_new,
        vector_step(expand_bias, expand_bias_grad, expand_bias_sum),
        shrink_weight_new,
        vector_step(shrink_bias, out_bias_grad, out_bias_grad),
        moments_new[0],
        moments_new[1].T,
        moments_new[2],
        moments_new[3].T,
    )


def solution(mesh):
    return jax.shard_map(
        shards,
        mesh=mesh,
        in_specs=(
            P(("dp", "tensor"), None),
            P(("dp", "tensor"), None),
            P("dp"),
            P(),
            P(),
            P(),
            P(),
            P("dp", "tensor"),
            P("tensor"),
            P("tensor", "dp"),
            P(),
            P("dp", "tensor"),
            P("tensor"),
            P("tensor", "dp"),
            P(),
            P("dp", "tensor"),
            P("tensor", "dp"),
            P("dp", "tensor"),
            P("tensor", "dp"),
        ),
        out_specs=(
            P(("dp", "tensor"), None),
            P(("dp", "tensor"), None),
            P(),
            P(),
            P(),
            P(),
            P("dp", "tensor"),
            P("tensor"),
            P("tensor", "dp"),
            P(),
            P("dp", "tensor"),
            P("tensor"),
            P("tensor", "dp"),
            P(),
            P(),
            P(),
            P(),
            P(),
            P("dp", "tensor"),
            P("tensor"),
            P("tensor", "dp"),
            P(),
            P("dp", "tensor"),
            P("tensor"),
            P("tensor", "dp"),
            P(),
            P("dp", "tensor"),
            P("tensor", "dp"),
            P("dp", "tensor"),
            P("tensor", "dp"),
        ),
        check_vma=False,
    )
```
